32 devices in a mesh: row: 4 (over x, core), col: 8 (over z, y).
Axes of the slice: x: 2, y: 2, z: 4, core: 2. Of those that a mesh axis runs over, the one named last changes fastest.
Arguments:
- node_features: bfloat16 [4096, 256], P(('row', 'col')), may hold values from -6 to 6
- layer_weight: bfloat16 [256, 256], replicated, may hold values from -0.375 to 0.375
- output_grad: bfloat16 [4096, 256], P(('row', 'col')), may hold values from -6 to 6
- block_values: bfloat16 [4, 8, 24, 128, 128], P('row', 'col'), may hold values from -0.15625 to 0.15625
- block_position: int32 [4, 8, 24], P('row', 'col'), may hold values from 0 to 31, as said below
- tile_count: int32 [4, 8], P('row', 'col'), may hold values from 6 to 24, as said below
Outputs:
- node_output: bfloat16 [4096, 256], P(('row', 'col'))
- input_grad: bfloat16 [4096, 256], P(('row', 'col'))
- weight_grad: float32 [256, 256], replicated
The draws below stay inside these ranges and needn't reach their ends.
Inputs may be any that keep to these rules, and one draw needn't show every extreme that they name: Tile (r, c) uses its slots 0 to tile_count[r, c] - 1; in every draw some tile uses all 24 slots. `block_position`: the slots of a tile hold distinct positions in increasing order.
All inputs are finite; a program needn't handle non-finite values.
Results may differ from the reference program's by a relative error of at most 0.02.
Values may be sent and summed in bfloat16 or wider, within the bound.
A program may use at most 64 MiB of HBM per device.

```python
import math
import jax
import jax.numpy as jnp
from jax import lax

WIDTH = 256
BLOCK = 128
NODE_DEV = 128
GRID_ROWS = 4
GRID_COLS = 8
ROW_PANEL = 1024
COL_PANEL = 512
ROW_BLOCKS = 8
COL_BLOCKS = 4
SLOTS = 24
NODES = 4096


def draw_block_position(key, part):
    tile_keys = jax.random.split(jax.random.fold_in(key, 7), GRID_ROWS * GRID_COLS)

    def one_tile(tile_key):
        shuffled = jax.random.permutation(tile_key, ROW_BLOCKS * COL_BLOCKS)
        return jnp.sort(shuffled[:SLOTS])
    chosen = jax.vmap(one_tile)(tile_keys)
    return chosen.reshape(GRID_ROWS, GRID_COLS, SLOTS).astype(jnp.int32)


def draw_tile_count(key, part):
    first_key = jax.random.fold_in(key, 11)
    second_key = jax.random.fold_in(key, 12)
    third_key = jax.random.fold_in(key, 13)
    base_count = jax.random.randint(first_key, (GRID_ROWS, GRID_COLS), SLOTS // 4, SLOTS // 2 + 1)
    heavy_tile = jax.random.randint(second_key, (GRID_ROWS, GRID_COLS), 0, 8) == 0
    counts = jnp.where(heavy_tile, SLOTS, base_count).reshape(-1)
    chosen_tile = jax.random.randint(third_key, (), 0, GRID_ROWS * GRID_COLS)
    counts = counts.at[chosen_tile].set(SLOTS)
    return counts.reshape(GRID_ROWS, GRID_COLS).astype(jnp.int32)


def block_levels(key, extent, cuts, low, high):
    def one(dim, blocks):
        heights = jax.random.uniform(jax.random.fold_in(jax.random.fold_in(key, 6), dim), (blocks,), jnp.float32, low / len(cuts), high / len(cuts))
        return jnp.repeat(jnp.exp(heights), extent[dim] // blocks).reshape((-1,) + (1,) * (len(extent) - dim - 1))

    factor_of = one(*cuts[0])
    for cut in cuts[1:]:
        factor_of = factor_of * one(*cut)
    return factor_of


def scatter_about(own_key, extent, deviation, reach, shards=(), kind=jnp.bfloat16):
    level = block_levels(own_key, extent, shards, -0.22, 0.18) if shards else 1.0
    array = jax.random.normal(own_key, extent, jnp.float32) * deviation * level
    return jnp.minimum(jnp.maximum(array, -reach), reach).astype(kind)


def setup_inputs(seed: int = 0) -> dict:
    streams_of = jax.random.split(jax.random.key(seed), 7)
    node_features = scatter_about(streams_of[0], (NODES, WIDTH), 1.0, 6.0, ((0, 32),))
    layer_weight = scatter_about(streams_of[1], (WIDTH, WIDTH), WIDTH ** -0.5, 0.375)
    output_grad = scatter_about(streams_of[2], (NODES, WIDTH), 1.0, 6.0, ((0, 32),))
    block_values = scatter_about(streams_of[3], (GRID_ROWS, GRID_COLS, SLOTS, BLOCK, BLOCK), (SLOTS * BLOCK * BLOCK // (2 * NODE_DEV)) ** -0.5, 0.15625, ((0, 4), (1, 8)))
    block_position = draw_block_position(jax.random.fold_in(streams_of[6], 71), 0)
    tile_count = draw_tile_count(jax.random.fold_in(streams_of[6], 71), 0)
    return dict(node_features=node_features, layer_weight=layer_weight, output_grad=output_grad, block_values=block_values, block_position=block_position, tile_count=tile_count)


def elu_slope(pre_activation):
    return jnp.where(pre_activation > 0, 1.0, jnp.exp(jnp.minimum(pre_activation, 0.0)))

def rounded(partial_value):
    return lax.optimization_barrier(partial_value.astype(jnp.bfloat16)).astype(jnp.float32)

def forward_tile(values, position, count, panel_rows):
    block_row = position // COL_BLOCKS
    block_col = position % COL_BLOCKS
    live = (jnp.arange(SLOTS, dtype=jnp.int32) < count).astype(jnp.float32)
    picked = panel_rows.reshape(COL_BLOCKS, BLOCK, WIDTH)[block_col]
    product = jnp.einsum('nij,njf->nif', values.astype(jnp.float32), picked.astype(jnp.float32))
    product = product * live[:, None, None]
    summed = jax.ops.segment_sum(product, block_row, num_segments=ROW_BLOCKS)
    return summed.reshape(ROW_PANEL, WIDTH)

def backward_tile(values, position, count, panel_rows):
    block_row = position // COL_BLOCKS
    block_col = position % COL_BLOCKS
    live = (jnp.arange(SLOTS, dtype=jnp.int32) < count).astype(jnp.float32)
    picked = panel_rows.reshape(ROW_BLOCKS, BLOCK, WIDTH)[block_row]
    product = jnp.einsum('nij,nif->njf', values.astype(jnp.float32), picked.astype(jnp.float32))
    product = product * live[:, None, None]
    summed = jax.ops.segment_sum(product, block_col, num_segments=COL_BLOCKS)
    return summed.reshape(COL_PANEL, WIDTH)

def reference(node_features, layer_weight, output_grad, block_values, block_position, tile_count):
    projected = jnp.dot(node_features, layer_weight, preferred_element_type=jnp.float32).astype(jnp.bfloat16)
    grid_view = projected.reshape(GRID_ROWS, GRID_COLS, NODE_DEV, WIDTH)
    col_panels = jnp.transpose(grid_view, (1, 0, 2, 3)).reshape(GRID_COLS, COL_PANEL, WIDTH)

    def row_sum(row_index):

        def add_tile(running, col_index):
            part = forward_tile(block_values[row_index, col_index], block_position[row_index, col_index], tile_count[row_index, col_index], col_panels[col_index])
            return (running + rounded(part), None)
        running, unused = lax.scan(add_tile, jnp.zeros((ROW_PANEL, WIDTH), jnp.float32), jnp.arange(GRID_COLS, dtype=jnp.int32))
        return running
    pre_activation = lax.map(row_sum, jnp.arange(GRID_ROWS, dtype=jnp.int32)).reshape(NODES, WIDTH)
    node_output = jax.nn.elu(pre_activation).astype(jnp.bfloat16)
    upstream = (output_grad.astype(jnp.float32) * elu_slope(pre_activation)).astype(jnp.bfloat16)
    row_panels = upstream.reshape(GRID_ROWS, ROW_PANEL, WIDTH)

    def col_sum(col_index):

        def add_tile(running, row_index):
            part = backward_tile(block_values[row_index, col_index], block_position[row_index, col_index], tile_count[row_index, col_index], row_panels[row_index])
            return (running + rounded(part), None)
        running, unused = lax.scan(add_tile, jnp.zeros((COL_PANEL, WIDTH), jnp.float32), jnp.arange(GRID_ROWS, dtype=jnp.int32))
        return running
    col_grads = lax.map(col_sum, jnp.arange(GRID_COLS, dtype=jnp.int32))
    column_grad = jnp.transpose(col_grads.reshape(GRID_COLS, GRID_ROWS, NODE_DEV, WIDTH), (1, 0, 2, 3))
    column_grad = column_grad.reshape(NODES, WIDTH)
    input_grad = jnp.dot(column_grad, layer_weight.astype(jnp.float32).T, precision=lax.Precision.HIGHEST).astype(jnp.bfloat16)
    weight_grad = jnp.dot(node_features.astype(jnp.float32).T, column_grad, precision=lax.Precision.HIGHEST) * (1.0 / math.sqrt(NODES))
    return (node_output, input_grad, weight_grad)
```

```python
import functools
import math

import jax
import jax.numpy as jnp
from jax import lax
from jax.experimental import pallas as pl
from jax.experimental.pallas import tpu as pltpu
from jax.sharding import PartitionSpec as P

MESH = pl.DeviceIdType.MESH
F32 = jnp.float32
BF16 = jnp.bfloat16
PARTS = 2
FEATS = 2


def repeat(steps, step):
    if len(steps) <= 8:
        for d in steps:
            step(d)
    elif len(steps) > 0:

        def one(d, unused):
            step(d)
            return unused

        lax.fori_loop(min(steps), max(steps) + 1, one, 0)


def split_dot(left, right, dims):
    high = left.astype(BF16)
    low = (left - high.astype(F32)).astype(BF16)
    first = lax.dot_general(high, right, dims, preferred_element_type=F32)
    return first + lax.dot_general(low, right, dims, preferred_element_type=F32)


def counts(rows, cols):
    half = cols // 2
    return {
        "load": 6,
        "x_mate": 1,
        "x_lead": 1,
        "x_rest": 1,
        "x_pass": 1,
        "ry": PARTS * half,
        "rz": PARTS,
        "gz": (1 + FEATS) * (half - 1),
        "gy": 1 + FEATS,
        "c_mate": FEATS,
        "c_pre": FEATS,
        "c_rest": FEATS,
        "c_lead": FEATS,
        "w": 3,
        "s_x": 1,
        "s_ry": 1,
        "s_rz": 1,
        "s_gz": 1,
        "s_gy": 1,
        "s_c": 1,
        "s_w": 3,
    }


def kernel(
    rows,
    cols,
    position_hbm,
    count_hbm,
    x_hbm,
    w_hbm,
    og_hbm,
    values_hbm,
    out_ref,
    ig_ref,
    wg_ref,
    position,
    count,
    values,
    w_ref,
    og_ref,
    xg,
    tile,
    tile_t,
    mate_part,
    mate_in,
    own,
    part,
    part_in,
    keep,
    up,
    acc,
    term_sum,
    term,
    w1_in,
    w2_in,
    w3_in,
    pc,
    pc_mate,
    pre_in,
    rest_in,
    lead_in,
    sems,
):
    scope = jax.named_scope
    nodes, width = x_hbm.shape
    slots, block = values_hbm.shape[0], values_hbm.shape[1]
    col_blocks = rows
    my_row = lax.axis_index("row")
    my_col = lax.axis_index("col")
    half = cols // 2
    exts = rows // 2
    high = my_col // 2
    low = lax.rem(my_col, 2)
    mate = high * 2 + 1 - low
    ext = my_row // 2
    core = lax.rem(my_row, 2)
    core_mate = ext * 2 + 1 - core
    plane = 2 * rows
    my_spot = my_row * 2 + low
    sub = nodes // PARTS
    fw = width // FEATS
    lead = nodes // 2
    rest = nodes - lead
    group = min(half, 4)
    groups = half // group
    others = [half // 2] + [d for d in range(1, half) if d != half // 2]
    ext_steps = list(range(1, exts))
    lead_rows, rest_rows = pl.ds(0, lead), pl.ds(lead, rest)

    base, at = {}, 0
    for name, size in counts(rows, cols).items():
        base[name] = at
        at += size

    def sem(name, index=0):
        return sems.at[base[name] + index]

    def high_ahead(d):
        return lax.rem(high + d, half)

    def high_behind(d):
        return lax.rem(high + half - d, half)

    def ext_ahead(d):
        return lax.rem(ext + d, exts)

    def ext_behind(d):
        return lax.rem(ext + exts - d, exts)

    def spot_ahead(d):
        return lax.rem(my_spot + d, plane)

    def move(src, dst, sent, got, **target):
        return pltpu.make_async_remote_copy(
            src_ref=src,
            dst_ref=dst,
            send_sem=sent,
            recv_sem=got,
            device_id=target,
            device_id_type=MESH,
        )

    def arrived(ref, got):
        move(ref, ref, sem("s_x"), got, col=mate).wait_recv()

    def gone(ref, sent):
        move(ref, ref, sent, sem("x_mate"), col=mate).wait_send()

    load = pltpu.make_async_copy(values_hbm, values.at[pl.ds(0, slots)], sem("load", 0))
    load_x = pltpu.make_async_copy(x_hbm, xg.at[my_row], sem("load", 1))
    load_w = pltpu.make_async_copy(w_hbm, w_ref, sem("load", 2))
    load_og = pltpu.make_async_copy(og_hbm, og_ref, sem("load", 3))
    load_position = pltpu.make_async_copy(position_hbm, position, sem("load", 4))
    load_count = pltpu.make_async_copy(count_hbm, count, sem("load", 5))
    for one in (load_x, load_position, load_count, load, load_w, load_og):
        one.start()

    barrier = pltpu.get_barrier_semaphore()

    def greet(**target):
        pl.semaphore_signal(barrier, inc=1, device_id=target, device_id_type=MESH)

    repeat(others, lambda d: greet(col=high_ahead(d) * 2 + low))

    def greet_spot(d):
        spot = spot_ahead(d)
        greet(row=spot // 2, col=high * 2 + lax.rem(spot, 2))

    repeat(list(range(1, plane)), greet_spot)
    values[slots] = jnp.zeros((block, block), BF16)
    load_x.wait()
    with scope("bar"):
        pl.semaphore_wait(barrier, plane - 1 + half - 1)

    mine = xg.at[my_row]

    def x_lead(d):
        move(
            mine.at[lead_rows], xg.at[my_row, lead_rows], sem("s_x"), sem("x_lead"),
            row=ext_ahead(d) * 2 + core,
        ).start()

    def x_rest(d):
        for to in (core, 1 - core):
            move(
                mine.at[rest_rows], xg.at[my_row, rest_rows], sem("s_x"), sem("x_rest"),
                row=ext_ahead(d) * 2 + to,
            ).start()

    repeat(ext_steps, x_lead)
    move(mine, mine, sem("s_x"), sem("x_mate"), row=core_mate).start()
    repeat(ext_steps, x_rest)

    with scope("load"):
        load_position.wait()
        load_count.wait()
        load.wait()
    live_count = count[0, 0]

    def build(q, y, z, pointer):
        for k in range(col_blocks):
            here = position[jnp.minimum(pointer, slots - 1)]
            live = (here == q * col_blocks + k) & (pointer < live_count)
            value = values[jnp.where(live, pointer, slots)]
            for p in range(PARTS):
                tile[p, y, z, :, pl.ds(k * block, block)] = value[p * sub : (p + 1) * sub, :]
            pointer = pointer + live.astype(jnp.int32)
        return pointer

    with scope("build"):
        if cols <= 8:
            pointer = jnp.int32(0)
            for q in range(cols):
                pointer = build(q, q % 2, q // 2, pointer)
        else:

            def build_pair(z, pointer):
                for y in range(2):
                    pointer = build(z * 2 + y, y, z, pointer)
                return pointer

            lax.fori_loop(0, half, build_pair, jnp.int32(0))

    with scope("x_lead"):
        arrived(xg.at[pl.ds(0, exts - 1), lead_rows], sem("x_lead"))

    def x_pass(d):
        slot = xg.at[ext_behind(d) * 2 + core, lead_rows]
        move(slot, slot, sem("s_x"), sem("x_pass"), row=core_mate).start()

    repeat(ext_steps, x_pass)
    with scope("x_rest"):
        arrived(xg.at[0], sem("x_mate"))
        arrived(xg.at[pl.ds(0, 2 * (exts - 1)), rest_rows], sem("x_rest"))
    with scope("x_pass"):
        arrived(xg.at[pl.ds(0, exts - 1), lead_rows], sem("x_pass"))

    depth = rows * nodes

    def product(p, y, g):
        left = tile[p, y, pl.ds(g * group, group)].reshape(group * sub, depth)
        panel = xg[...].reshape(depth, width)
        return jnp.dot(left, panel, preferred_element_type=F32).reshape(group, sub, width)

    def for_mate(p):
        def one(g):
            mate_part[p, pl.ds(g * group, group)] = product(p, 1 - low, g).astype(BF16)

        repeat_all(groups, one)

        def send(d):
            z = high_ahead(d)
            move(
                mate_part.at[p, z], mate_in.at[p, z], sem("s_ry"), sem("ry", p * half + d), col=mate
            ).start()

        repeat(others, send)
        send(0)

    def for_me(p):
        def one(g):
            own[p, pl.ds(g * group, group)] = product(p, low, g)

        repeat_all(groups, one)

    def repeat_all(count, step):
        if count == 1:
            step(0)
        else:

            def one(g, unused):
                step(g)
                return unused

            lax.fori_loop(0, count, one, 0)

    with scope("fwd"):
        for p in range(PARTS):
            for_mate(p)
        for p in range(PARTS):
            for_me(p)

    def turn(p, y):
        def one(g):
            for k in range(col_blocks):
                left = tile[p, y, pl.ds(g * group, group), :, pl.ds(k * block, block)]
                tile_t[p, y, g, pl.ds(k * block, block), :] = left.reshape(group * sub, block).T

        repeat_all(groups, one)

    with scope("turn"):
        for p in range(PARTS):
            for y in range(2):
                turn(p, y)

    def to_high(p):
        def one(d):
            z = high_ahead(d)
            arrived(mate_in.at[p, z], sem("ry", p * half + d))
            part[p, z] = (own[p, z] + mate_in[p, z].astype(F32)).astype(BF16)
            move(
                part.at[p, z], part_in.at[p, high], sem("s_rz"), sem("rz", p), col=z * 2 + low
            ).start()

        repeat(others, one)
        arrived(mate_in.at[p, high], sem("ry", p * half))
        keep[p] = own[p, high] + mate_in[p, high].astype(F32)

    for p in range(PARTS):
        with scope("to_high%d" % p):
            to_high(p)

    load_w.wait()
    load_og.wait()
    scale = 1.0 / math.sqrt(nodes * rows * cols)
    piece = width // plane
    over_nodes = (((0,), (0,)), ((), ()))
    both = pl.ds(0, FEATS)

    def spread(f, p, index):
        mine = up.at[f, p, low, high]
        repeat(
            others,
            lambda d: move(
                mine, mine, sem("s_gz"), sem("gz", index * (half - 1) + d - 1),
                col=high_ahead(d) * 2 + low,
            ).start(),
        )
        move(mine, mine, sem("s_gy"), sem("gy", index), col=mate).start()

    def middle(p):
        with scope("rz%d" % p):
            arrived(part_in.at[p, pl.ds(0, half - 1)], sem("rz", p))

        def add(d):
            keep[p] += part_in[p, high_behind(d)].astype(F32)

        repeat(others, add)
        mixed = keep[p]
        pre = split_dot(mixed, w_ref[...], (((1,), (0,)), ((), ())))
        decay = jnp.exp(jnp.minimum(pre, 0.0))
        slope = jnp.where(pre > 0, 1.0, decay)
        some = pl.ds(p * sub, sub)
        upstream = (og_ref[some].astype(F32) * slope).astype(BF16)
        for f in range(FEATS):
            up[f, p, low, high] = upstream[:, f * fw : (f + 1) * fw]
        if p < PARTS - 1:
            spread(both, p, 0)
        else:
            for f in range(FEATS):
                spread(f, p, 1 + f)
        out_ref[some] = jnp.where(pre > 0, pre, decay - 1.0).astype(BF16)
        share = split_dot(mixed, upstream, over_nodes)
        if p == 0:
            term_sum[...] = share
        else:
            share = term_sum[...] + share
            term[...] = (share * scale).reshape(plane, piece, width).astype(BF16)

    for p in range(PARTS):
        with scope("middle%d" % p):
            middle(p)

    def to_spots(src, dst, sent, got):
        def one(d):
            spot = spot_ahead(d)
            move(
                src(spot), dst.at[my_spot], sent, got,
                row=spot // 2, col=high * 2 + lax.rem(spot, 2),
            ).start()

        repeat(list(range(1, plane)), one)

    with scope("w1_send"):
        to_spots(lambda spot: term.at[spot], w1_in, sem("s_w", 0), sem("w", 0))
        w1_in[my_spot] = term[my_spot]

    def region(f, p, z):
        return up.at[f, p, low, z]

    def pass_on(f, p, index):
        def one(d):
            slot = region(f, p, high_behind(d))
            arrived(slot, sem("gz", index * (half - 1) + d - 1))
            move(slot, slot, sem("s_gy"), sem("gy", index), col=mate).start()

        repeat(others, one)

    def back(f, p, y, first=False):
        def one(g):
            right = up[f, p, y, pl.ds(g * group, group)].reshape(group * sub, fw)
            got = jnp.dot(tile_t[p, y, g], right, preferred_element_type=F32)
            if first:
                acc[f] = got
            else:
                acc[f] += got

        if first and groups > 1:
            acc[f] = jnp.zeros(acc.shape[1:], F32)
            first = False
        repeat_all(groups, one)

    with scope("gz_p0"):
        pass_on(both, 0, 0)
    for f in range(FEATS):
        back(f, 0, low, first=True)
    for f in range(FEATS):
        with scope("gz_p1_%d" % f):
            pass_on(f, 1, 1 + f)
    with scope("w1_wait"):
        arrived(w1_in.at[pl.ds(0, plane - 1)], sem("w", 0))
        w2_in[high] = jnp.sum(w1_in[...].astype(F32), axis=0).astype(BF16)
        repeat(
            others,
            lambda d: move(
                w2_in.at[high], w2_in.at[high], sem("s_w", 1), sem("w", 1),
                col=high_ahead(d) * 2 + low,
            ).start(),
        )
    for f in range(FEATS):
        back(f, 1, low)

    with scope("gy_p0"):
        arrived(up.at[both, 0, 1 - low], sem("gy", 0))
    for f in range(FEATS):
        back(f, 0, 1 - low)

    def block_of(r):
        return pl.ds(pl.multiple_of(r * nodes, nodes), nodes)

    def lead_of(r):
        return pl.ds(pl.multiple_of(r * nodes, nodes), lead)

    def rest_of(r):
        return pl.ds(pl.multiple_of(r * nodes + lead, rest), rest)

    def launch(f):
        pc[f, core_mate] = acc[f, block_of(core_mate)].astype(BF16)

        def pre(d):
            far = ext_ahead(d)
            other = far * 2 + 1 - core
            pc[f, other] = acc[f, block_of(other)].astype(BF16)
            move(
                pc.at[f, other, lead_rows], pre_in.at[f, far], sem("s_c"), sem("c_pre", f),
                row=core_mate,
            ).start()

        repeat(ext_steps, pre)

        def direct(d):
            far = ext_ahead(d)
            same = far * 2 + core
            other = far * 2 + 1 - core
            move(
                pc.at[f, other, rest_rows], rest_in.at[f, my_row], sem("s_c"), sem("c_rest", f),
                row=other,
            ).start()
            pc[f, same, rest_rows] = acc[f, rest_of(same)].astype(BF16)
            move(
                pc.at[f, same, rest_rows], rest_in.at[f, my_row], sem("s_c"), sem("c_rest", f),
                row=same,
            ).start()

        repeat(ext_steps, direct)
        move(pc.at[f, core_mate], pc_mate.at[f], sem("s_c"), sem("c_mate", f), row=core_mate).start()

    def relay(f):
        arrived(pre_in.at[f, pl.ds(0, exts - 1)], sem("c_pre", f))

        def one(d):
            far = ext_ahead(d)
            same = far * 2 + core
            pc[f, same, lead_rows] = (
                acc[f, lead_of(same)] + pre_in[f, far].astype(F32)
            ).astype(BF16)
            move(
                pc.at[f, same, lead_rows], lead_in.at[f, ext], sem("s_c"), sem("c_lead", f),
                row=same,
            ).start()

        repeat(ext_steps, one)

    def gather_grad(f):
        arrived(pc_mate.at[f], sem("c_mate", f))
        acc[f, block_of(my_row)] += pc_mate[f].astype(F32)
        arrived(rest_in.at[f, pl.ds(0, 2 * (exts - 1))], sem("c_rest", f))

        def add_rest(d):
            for k in range(2):
                acc[f, rest_of(my_row)] += rest_in[f, ext_behind(d) * 2 + k].astype(F32)

        repeat(ext_steps, add_rest)
        arrived(lead_in.at[f, pl.ds(0, exts - 1)], sem("c_lead", f))

        def add_lead(d):
            acc[f, lead_of(my_row)] += lead_in[f, ext_behind(d)].astype(F32)

        repeat(ext_steps, add_lead)
        some = pl.ds(f * fw, fw)
        return split_dot(acc[f, block_of(my_row)], w_ref[:, some], (((1,), (1,)), ((), ())))

    for f in range(FEATS):
        with scope("gy_p1_%d" % f):
            arrived(up.at[f, 1, 1 - low], sem("gy", 1 + f))
        back(f, 1, 1 - low)
        with scope("launch%d" % f):
            launch(f)
        if f < FEATS - 1:
            with scope("relay%d" % f):
                relay(f)
    with scope("w2_wait"):
        arrived(w2_in.at[pl.ds(0, half - 1)], sem("w", 1))
        w3_in[my_spot] = jnp.sum(w2_in[...].astype(F32), axis=0).astype(BF16)
        to_spots(lambda spot: w3_in.at[my_spot], w3_in, sem("s_w", 2), sem("w", 2))
    with scope("relay_last"):
        relay(FEATS - 1)
    grad = 0.0
    for f in range(FEATS):
        with scope("grad%d" % f):
            grad = grad + gather_grad(f)
    ig_ref[...] = grad.astype(BF16)

    with scope("gone"):
        gone(xg.at[pl.ds(0, rows - 1)], sem("s_x"))
        gone(mate_part, sem("s_ry"))
        gone(part.at[:, pl.ds(0, half - 1)], sem("s_rz"))
        gone(up.at[:, :, low, pl.ds(0, half - 1)], sem("s_gz"))
        gone(up.at[:, :, low], sem("s_gy"))
        gone(pc.at[:, pl.ds(0, rows - 1)], sem("s_c"))
        gone(term.at[pl.ds(0, plane - 1)], sem("s_w", 0))
        gone(w2_in.at[pl.ds(0, half - 1)], sem("s_w", 1))
        gone(w3_in.at[pl.ds(0, plane - 1)], sem("s_w", 2))
    with scope("w3_wait"):
        arrived(w3_in.at[pl.ds(0, plane - 1)], sem("w", 2))
    wg_ref[...] = w3_in[...].reshape(width, width).astype(F32)


def finish(out_ref, ig_ref, wg_ref, out_hbm, ig_hbm, wg_hbm, sem):
    trio = ((out_ref, out_hbm), (ig_ref, ig_hbm), (wg_ref, wg_hbm))
    copies = [pltpu.make_async_copy(a, b, sem.at[i]) for i, (a, b) in enumerate(trio)]
    for copy in copies:
        copy.start()
    for copy in copies:
        copy.wait()


def body(node_features, layer_weight, output_grad, block_values, block_position, tile_count):
    rows, cols = lax.axis_size("row"), lax.axis_size("col")
    nodes, width = node_features.shape
    slots, block = block_values.shape[2], block_values.shape[3]
    half, exts, plane = cols // 2, rows // 2, 2 * rows
    assert nodes == block and cols == 2 * half and rows == 2 * exts
    sub, fw = nodes // PARTS, width // FEATS
    lead = nodes // 2
    rest = nodes - lead
    group = min(half, 4)
    groups = half // group
    piece = width // plane
    depth = rows * nodes
    place = pl.BlockSpec(memory_space=pl.ANY)
    pinned = pl.BlockSpec(memory_space=pltpu.HBM)
    inside = pl.BlockSpec(memory_space=pltpu.VMEM)
    dma = pltpu.SemaphoreType.DMA
    vmem = pltpu.VMEM
    shapes = (
        jax.ShapeDtypeStruct((nodes, width), BF16),
        jax.ShapeDtypeStruct((nodes, width), BF16),
        jax.ShapeDtypeStruct((width, width), F32),
    )
    results = pl.pallas_call(
        functools.partial(kernel, rows, cols),
        out_shape=(
            vmem((nodes, width), BF16),
            vmem((nodes, width), BF16),
            vmem((width, width), F32),
        ),
        in_specs=[pinned, pinned, place, place, place, place],
        out_specs=(inside, inside, inside),
        scratch_shapes=[
            pltpu.SMEM((slots,), jnp.int32),
            pltpu.SMEM((1, 1), jnp.int32),
            vmem((slots + 1, block, block), BF16),
            vmem((width, width), BF16),
            vmem((nodes, width), BF16),
            vmem((rows, nodes, width), BF16),
            vmem((PARTS, 2, half, sub, depth), BF16),
            vmem((PARTS, 2, groups, depth, group * sub), BF16),
            vmem((PARTS, half, sub, width), BF16),
            vmem((PARTS, half, sub, width), BF16),
            vmem((PARTS, half, sub, width), F32),
            vmem((PARTS, half, sub, width), BF16),
            vmem((PARTS, half, sub, width), BF16),
            vmem((PARTS, sub, width), F32),
            vmem((FEATS, PARTS, 2, half, sub, fw), BF16),
            vmem((FEATS, depth, fw), F32),
            vmem((width, width), F32),
            vmem((plane, piece, width), BF16),
            vmem((plane, piece, width), BF16),
            vmem((half, piece, width), BF16),
            vmem((plane, piece, width), BF16),
            vmem((FEATS, rows, nodes, fw), BF16),
            vmem((FEATS, nodes, fw), BF16),
            vmem((FEATS, exts, lead, fw), BF16),
            vmem((FEATS, rows, rest, fw), BF16),
            vmem((FEATS, exts, lead, fw), BF16),
            dma((sum(counts(rows, cols).values()),)),
        ],
        compiler_params=pltpu.CompilerParams(collective_id=0, has_side_effects=True),
    )(
        block_position.reshape(slots),
        tile_count,
        node_features,
        layer_weight,
        output_grad,
        block_values.reshape(slots, block, block),
    )
    return pl.pallas_call(
        finish,
        out_shape=shapes,
        in_specs=[inside] * 3,
        out_specs=(place,) * 3,
        scratch_shapes=[
            dma((3,)),
        ],
        compiler_params=pltpu.CompilerParams(vmem_limit_bytes=4 << 20),
    )(*results)


def solution(mesh):
    in_specs = (
        P(("row", "col"), None),
        P(),
        P(("row", "col"), None),
        P("row", "col", None, None, None),
        P("row", "col", None),
        P("row", "col"),
    )
    out_specs = (P(("row", "col"), None), P(("row", "col"), None), P())
    return jax.shard_map(body, mesh=mesh, in_specs=in_specs, out_specs=out_specs, check_vma=False)
```

```python
import functools
import math

import jax
import jax.numpy as jnp
from jax import lax
from jax.experimental import pallas as pl
from jax.experimental.pallas import tpu as pltpu
from jax.sharding import PartitionSpec as P

MESH = pl.DeviceIdType.MESH
F32 = jnp.float32
BF16 = jnp.bfloat16
PARTS = 2
FEATS = 2


def repeat(steps, step):
    if len(steps) <= 8:
        for d in steps:
            step(d)
    elif len(steps) > 0:

        def one(d, unused):
            step(d)
            return unused

        lax.fori_loop(min(steps), max(steps) + 1, one, 0)


def split_dot(left, right, dims):
    high = left.astype(BF16)
    low = (left - high.astype(F32)).astype(BF16)
    first = lax.dot_general(high, right, dims, preferred_element_type=F32)
    return first + lax.dot_general(low, right, dims, preferred_element_type=F32)


def counts(rows, cols):
    half = cols // 2
    return {
        "load": 5 + FEATS,
        "x_mate": FEATS,
        "x_lead": FEATS,
        "x_rest": FEATS,
        "x_pass": FEATS,
        "yc": PARTS * FEATS * (half // 2),
        "yb": PARTS * (half // 2),
        "rz": PARTS,
        "gz": (1 + FEATS) * (half - 1),
        "gy": 1 + FEATS,
        "c": FEATS,
        "w": 3,
        "s_x": 1,
        "s_ry": 1,
        "s_rz": 1,
        "s_gz": 1,
        "s_gy": 1,
        "s_c": 1,
        "s_w": 3,
    }


def kernel(
    rows,
    cols,
    position_hbm,
    count_hbm,
    x_hbm,
    w_hbm,
    og_hbm,
    values_hbm,
    out_ref,
    ig_ref,
    wg_ref,
    position,
    count,
    values,
    w_ref,
    og_ref,
    xg,
    tile,
    tile_t,
    mate_part,
    mate_in,
    own,
    part,
    part_in,
    keep,
    up,
    acc,
    term_sum,
    term,
    w1_in,
    w2_in,
    w3_in,
    pc,
    pc_in,
    sems,
):
    scope = jax.named_scope
    nodes, width = x_hbm.shape
    slots, block = values_hbm.shape[0], values_hbm.shape[1]
    col_blocks = rows
    my_row = lax.axis_index("row")
    my_col = lax.axis_index("col")
    half = cols // 2
    exts = rows // 2
    high = my_col // 2
    low = lax.rem(my_col, 2)
    mate = high * 2 + 1 - low
    ext = my_row // 2
    core = lax.rem(my_row, 2)
    core_mate = ext * 2 + 1 - core
    plane = 2 * rows
    my_spot = my_row * 2 + low
    sub = nodes // PARTS
    fw = width // FEATS
    lead = nodes // 2
    rest = nodes - lead
    group = min(half, 4)
    groups = half // group
    wing = half // 2
    side = high // wing
    rank = lax.rem(high, wing)
    ext_steps = list(range(1, exts))
    lead_rows, rest_rows = pl.ds(0, lead), pl.ds(lead, rest)

    base, at = {}, 0
    for name, size in counts(rows, cols).items():
        base[name] = at
        at += size

    def sem(name, index=0):
        return sems.at[base[name] + index]

    def across(step):
        def one(j):
            far = (1 - side) * wing + lax.rem(wing - 1 - rank + j, wing)
            step(j, far, far)

        repeat(list(range(wing)), one)

    def beside(step):
        def one(j):
            to = side * wing + lax.rem(rank + j, wing)
            come = side * wing + lax.rem(rank + wing - j, wing)
            step(wing - 1 + j, to, come)

        repeat(list(range(1, wing)), one)

    def far_first(step):
        across(step)
        beside(step)

    def near_first(step):
        beside(step)
        across(step)

    def ext_ahead(d):
        return lax.rem(ext + d, exts)

    def ext_behind(d):
        return lax.rem(ext + exts - d, exts)

    def spot_ahead(d):
        return lax.rem(my_spot + d, plane)

    def move(src, dst, sent, got, **target):
        return pltpu.make_async_remote_copy(
            src_ref=src,
            dst_ref=dst,
            send_sem=sent,
            recv_sem=got,
            device_id=target,
            device_id_type=MESH,
        )

    def arrived(ref, got):
        move(ref, ref, sem("s_x"), got, col=mate).wait_recv()

    def gone(ref, sent):
        move(ref, ref, sent, sem("x_mate"), col=mate).wait_send()

    load = pltpu.make_async_copy(values_hbm, values.at[pl.ds(0, slots)], sem("load", 0))
    load_x = [
        pltpu.make_async_copy(
            x_hbm.at[:, pl.ds(f * fw, fw)], xg.at[f, my_row], sem("load", 5 + f)
        )
        for f in range(FEATS)
    ]
    load_w = pltpu.make_async_copy(w_hbm, w_ref, sem("load", 2))
    load_og = pltpu.make_async_copy(og_hbm, og_ref, sem("load", 3))
    load_position = pltpu.make_async_copy(position_hbm, position, sem("load", 4))
    load_count = pltpu.make_async_copy(count_hbm, count, sem("load", 1))
    for one in (*load_x, load_position, load_count, load, load_w, load_og):
        one.start()

    barrier = pltpu.get_barrier_semaphore()

    def greet(**target):
        pl.semaphore_signal(barrier, inc=1, device_id=target, device_id_type=MESH)

    far_first(lambda t, to, come: greet(col=to * 2 + low))

    def greet_spot(d):
        spot = spot_ahead(d)
        greet(row=spot // 2, col=high * 2 + lax.rem(spot, 2))

    repeat(list(range(1, plane)), greet_spot)
    values[slots] = jnp.zeros((block, block), BF16)
    for one in load_x:
        one.wait()
    with scope("bar"):
        pl.semaphore_wait(barrier, plane - 1 + half - 1)

    def x_send(f):
        mine = xg.at[f, my_row]

        def send_lead(d):
            move(
                mine.at[lead_rows], mine.at[lead_rows], sem("s_x"), sem("x_lead", f),
                row=ext_ahead(d) * 2 + core,
            ).start()

        def send_rest(d):
            for to in (core, 1 - core):
                move(
                    mine.at[rest_rows], mine.at[rest_rows], sem("s_x"), sem("x_rest", f),
                    row=ext_ahead(d) * 2 + to,
                ).start()

        repeat(ext_steps, send_lead)
        move(mine, mine, sem("s_x"), sem("x_mate", f), row=core_mate).start()
        repeat(ext_steps, send_rest)

    x_send(0)

    with scope("load"):
        load_position.wait()
        load_count.wait()
        load.wait()
    live_count = count[0, 0]

    def build(q, y, z, pointer):
        for k in range(col_blocks):
            here = position[jnp.minimum(pointer, slots - 1)]
            live = (here == q * col_blocks + k) & (pointer < live_count)
            value = values[jnp.where(live, pointer, slots)]
            for p in range(PARTS):
                tile[p, y, z, :, pl.ds(k * block, block)] = value[p * sub : (p + 1) * sub, :]
            pointer = pointer + live.astype(jnp.int32)
        return pointer

    with scope("build"):
        if cols <= 8:
            pointer = jnp.int32(0)
            for q in range(cols):
                pointer = build(q, q % 2, q // 2, pointer)
        else:

            def build_pair(z, pointer):
                for y in range(2):
                    pointer = build(z * 2 + y, y, z, pointer)
                return pointer

            lax.fori_loop(0, half, build_pair, jnp.int32(0))

    for f in range(1, FEATS):
        x_send(f)

    depth = rows * nodes

    def x_relay(f):
        with scope("x_lead%d" % f):
            arrived(xg.at[f, pl.ds(0, exts - 1), lead_rows], sem("x_lead", f))

        def one(d):
            slot = xg.at[f, ext_behind(d) * 2 + core, lead_rows]
            move(slot, slot, sem("s_x"), sem("x_pass", f), row=core_mate).start()

        repeat(ext_steps, one)

    def x_wait(f):
        with scope("x_rest%d" % f):
            arrived(xg.at[f, 0], sem("x_mate", f))
            arrived(xg.at[f, pl.ds(0, 2 * (exts - 1)), rest_rows], sem("x_rest", f))
        with scope("x_pass%d" % f):
            arrived(xg.at[f, pl.ds(0, exts - 1), lead_rows], sem("x_pass", f))

    def repeat_all(count, step):
        if count == 1:
            step(0)
        else:

            def one(g, unused):
                step(g)
                return unused

            lax.fori_loop(0, count, one, 0)

    def product(p, f, y, g):
        left = tile[p, y, pl.ds(g * group, group)].reshape(group * sub, depth)
        panel = xg[f].reshape(depth, fw)
        return jnp.dot(left, panel, preferred_element_type=F32).reshape(group, sub, fw)

    def yc(p, f, j):
        return sem("yc", (p * FEATS + f) * wing + j)

    def yb(p, j):
        return sem("yb", p * wing + j)

    def for_mate(p, f):
        def one(g):
            mate_part[p, f, pl.ds(g * group, group)] = product(p, f, 1 - low, g).astype(BF16)

        repeat_all(groups, one)

        def send(j, z, unused):
            move(
                mate_part.at[p, f, z], mate_in.at[p, f, z], sem("s_ry"), yc(p, f, j), col=mate
            ).start()

        across(send)

    def for_mate_near(p):
        def send(t, z, unused):
            move(
                mate_part.at[p, :, z], mate_in.at[p, :, z], sem("s_ry"), yb(p, t - wing), col=mate
            ).start()

        beside(send)
        send(2 * wing - 1, high, high)

    def for_me(p, f):
        def one(g):
            own[p, f, pl.ds(g * group, group)] = product(p, f, low, g)

        repeat_all(groups, one)

    x_relay(0)
    x_wait(0)
    with scope("fwd0"):
        for_mate(0, 0)
    for f in range(1, FEATS):
        x_relay(f)
    for f in range(1, FEATS):
        x_wait(f)
        for_mate(0, f)
    with scope("fwd1"):
        for p in range(1, PARTS):
            for f in range(FEATS):
                for_mate(p, f)
        for p in range(PARTS):
            for_mate_near(p)
        for p in range(PARTS):
            for f in range(FEATS):
                for_me(p, f)

    def turn(p, y):
        def one(g):
            for k in range(col_blocks):
                left = tile[p, y, pl.ds(g * group, group), :, pl.ds(k * block, block)]
                tile_t[p, y, g, pl.ds(k * block, block), :] = left.reshape(group * sub, block).T

        repeat_all(groups, one)

    with scope("turn"):
        for p in range(PARTS):
            for y in range(2):
                turn(p, y)

    def to_across(p, f):
        def one(j, z, unused):
            arrived(mate_in.at[p, f, z], yc(p, f, j))
            part[p, f, z] = (own[p, f, z] + mate_in[p, f, z].astype(F32)).astype(BF16)
            move(
                part.at[p, f, z], part_in.at[p, f, high], sem("s_rz"), sem("rz", p),
                col=z * 2 + low,
            ).start()

        across(one)

    def to_beside(p):
        def one(t, z, unused):
            arrived(mate_in.at[p, :, z], yb(p, t - wing))
            part[p, :, z] = (own[p, :, z] + mate_in[p, :, z].astype(F32)).astype(BF16)
            move(
                part.at[p, :, z], part_in.at[p, :, high], sem("s_rz"), sem("rz", p),
                col=z * 2 + low,
            ).start()

        beside(one)
        arrived(mate_in.at[p, :, high], yb(p, wing - 1))
        keep[p] = own[p, :, high] + mate_in[p, :, high].astype(F32)

    for p in range(PARTS):
        for f in range(FEATS):
            with scope("across%d%d" % (p, f)):
                to_across(p, f)
    for p in range(PARTS):
        with scope("beside%d" % p):
            to_beside(p)

    load_w.wait()
    load_og.wait()
    scale = 1.0 / math.sqrt(nodes * rows * cols)
    piece = width // plane
    over_nodes = (((0,), (0,)), ((), ()))
    both = pl.ds(0, FEATS)

    def spread(f, p, index):
        mine = up.at[f, p, low, high]
        far_first(
            lambda t, z, unused: move(
                mine, mine, sem("s_gz"), sem("gz", index * (half - 1) + t), col=z * 2 + low
            ).start()
        )
        move(mine, mine, sem("s_gy"), sem("gy", index), col=mate).start()

    def middle(p):
        with scope("rz%d" % p):
            arrived(part_in.at[p, :, pl.ds(0, half - 1)], sem("rz", p))

        def add(t, unused, z):
            keep[p] += part_in[p, :, z].astype(F32)

        near_first(add)
        mixed = jnp.concatenate([keep[p, f] for f in range(FEATS)], axis=1)
        pre = split_dot(mixed, w_ref[...], (((1,), (0,)), ((), ())))
        decay = jnp.exp(jnp.minimum(pre, 0.0))
        slope = jnp.where(pre > 0, 1.0, decay)
        some = pl.ds(p * sub, sub)
        upstream = (og_ref[some].astype(F32) * slope).astype(BF16)
        for f in range(FEATS):
            up[f, p, low, high] = upstream[:, f * fw : (f + 1) * fw]
        if p < PARTS - 1:
            spread(both, p, 0)
        else:
            for f in range(FEATS):
                spread(f, p, 1 + f)
        out_ref[some] = jnp.where(pre > 0, pre, decay - 1.0).astype(BF16)
        share = split_dot(mixed, upstream, over_nodes)
        if p == 0:
            term_sum[...] = share
        else:
            share = term_sum[...] + share
            term[...] = (share * scale).reshape(plane, piece, width).astype(BF16)

    for p in range(PARTS):
        with scope("middle%d" % p):
            middle(p)

    def to_spots(src, dst, sent, got):
        def one(d):
            spot = spot_ahead(d)
            move(
                src(spot), dst.at[my_spot], sent, got,
                row=spot // 2, col=high * 2 + lax.rem(spot, 2),
            ).start()

        repeat(list(range(1, plane)), one)

    with scope("w1_send"):
        to_spots(lambda spot: term.at[spot], w1_in, sem("s_w", 0), sem("w", 0))
        w1_in[my_spot] = term[my_spot]

    def region(f, p, z):
        return up.at[f, p, low, z]

    def pass_on(f, p, index):
        def one(t, unused, z):
            slot = region(f, p, z)
            arrived(slot, sem("gz", index * (half - 1) + t))
            move(slot, slot, sem("s_gy"), sem("gy", index), col=mate).start()

        near_first(one)

    def back(f, p, y, first=False):
        def one(g):
            right = up[f, p, y, pl.ds(g * group, group)].reshape(group * sub, fw)
            got = jnp.dot(tile_t[p, y, g], right, preferred_element_type=F32)
            if first:
                acc[f] = got
            else:
                acc[f] += got

        if first and groups > 1:
            acc[f] = jnp.zeros(acc.shape[1:], F32)
            first = False
        repeat_all(groups, one)

    with scope("gz_p0"):
        pass_on(both, 0, 0)
    for f in range(FEATS):
        back(f, 0, low, first=True)
    for f in range(FEATS):
        with scope("gz_p1_%d" % f):
            pass_on(f, 1, 1 + f)
    with scope("w1_wait"):
        arrived(w1_in.at[pl.ds(0, plane - 1)], sem("w", 0))
        w2_in[high] = jnp.sum(w1_in[...].astype(F32), axis=0).astype(BF16)
        far_first(
            lambda t, z, unused: move(
                w2_in.at[high], w2_in.at[high], sem("s_w", 1), sem("w", 1), col=z * 2 + low
            ).start()
        )
    for f in range(FEATS):
        back(f, 1, low)

    with scope("gy_p0"):
        arrived(up.at[both, 0, 1 - low], sem("gy", 0))
    for f in range(FEATS):
        back(f, 0, 1 - low)

    def block_of(r):
        return pl.ds(pl.multiple_of(r * nodes, nodes), nodes)

    def launch(f):
        def one(r):
            pc[f, r] = acc[f, block_of(r)].astype(BF16)
            move(pc.at[f, r], pc_in.at[f, my_row], sem("s_c"), sem("c", f), row=r).start()

        def outside(d):
            one(ext_ahead(d) * 2 + core)
            one(ext_ahead(d) * 2 + 1 - core)

        repeat(ext_steps, outside)
        one(core_mate)

    def gather_grad(f):
        arrived(pc_in.at[f, pl.ds(0, rows - 1)], sem("c", f))

        def add(r):
            acc[f, block_of(my_row)] += pc_in[f, r].astype(F32)

        def outside(d):
            for k in range(2):
                add(ext_behind(d) * 2 + k)

        repeat(ext_steps, outside)
        add(core_mate)
        some = pl.ds(f * fw, fw)
        return split_dot(acc[f, block_of(my_row)], w_ref[:, some], (((1,), (1,)), ((), ())))

    for f in range(FEATS):
        with scope("gy_p1_%d" % f):
            arrived(up.at[f, 1, 1 - low], sem("gy", 1 + f))
        back(f, 1, 1 - low)
        with scope("launch%d" % f):
            launch(f)
    with scope("w2_wait"):
        arrived(w2_in.at[pl.ds(0, half - 1)], sem("w", 1))
        w3_in[my_spot] = jnp.sum(w2_in[...].astype(F32), axis=0).astype(BF16)
        to_spots(lambda spot: w3_in.at[my_spot], w3_in, sem("s_w", 2), sem("w", 2))
    grad = 0.0
    for f in range(FEATS):
        with scope("grad%d" % f):
            grad = grad + gather_grad(f)
    ig_ref[...] = grad.astype(BF16)

    with scope("gone"):
        gone(xg.at[:, pl.ds(0, rows - 1)], sem("s_x"))
        gone(mate_part, sem("s_ry"))
        gone(part.at[:, :, pl.ds(0, half - 1)], sem("s_rz"))
        gone(up.at[:, :, low, pl.ds(0, half - 1)], sem("s_gz"))
        gone(up.at[:, :, low], sem("s_gy"))
        gone(pc.at[:, pl.ds(0, rows - 1)], sem("s_c"))
        gone(term.at[pl.ds(0, plane - 1)], sem("s_w", 0))
        gone(w2_in.at[pl.ds(0, half - 1)], sem("s_w", 1))
        gone(w3_in.at[pl.ds(0, plane - 1)], sem("s_w", 2))
    with scope("w3_wait"):
        arrived(w3_in.at[pl.ds(0, plane - 1)], sem("w", 2))
    wg_ref[...] = w3_in[...].reshape(width, width).astype(F32)


def finish(out_ref, ig_ref, wg_ref, out_hbm, ig_hbm, wg_hbm, sem):
    trio = ((out_ref, out_hbm), (ig_ref, ig_hbm), (wg_ref, wg_hbm))
    copies = [pltpu.make_async_copy(a, b, sem.at[i]) for i, (a, b) in enumerate(trio)]
    for copy in copies:
        copy.start()
    for copy in copies:
        copy.wait()


def body(node_features, layer_weight, output_grad, block_values, block_position, tile_count):
    rows, cols = lax.axis_size("row"), lax.axis_size("col")
    nodes, width = node_features.shape
    slots, block = block_values.shape[2], block_values.shape[3]
    half, exts, plane = cols // 2, rows // 2, 2 * rows
    assert nodes == block and cols == 2 * half and rows == 2 * exts
    sub, fw = nodes // PARTS, width // FEATS
    lead = nodes // 2
    rest = nodes - lead
    group = min(half, 4)
    groups = half // group
    piece = width // plane
    depth = rows * nodes
    place = pl.BlockSpec(memory_space=pl.ANY)
    pinned = pl.BlockSpec(memory_space=pltpu.HBM)
    inside = pl.BlockSpec(memory_space=pltpu.VMEM)
    dma = pltpu.SemaphoreType.DMA
    vmem = pltpu.VMEM
    shapes = (
        jax.ShapeDtypeStruct((nodes, width), BF16),
        jax.ShapeDtypeStruct((nodes, width), BF16),
        jax.ShapeDtypeStruct((width, width), F32),
    )
    results = pl.pallas_call(
        functools.partial(kernel, rows, cols),
        out_shape=(
            vmem((nodes, width), BF16),
            vmem((nodes, width), BF16),
            vmem((width, width), F32),
        ),
        in_specs=[pinned, pinned, place, place, place, place],
        out_specs=(inside, inside, inside),
        scratch_shapes=[
            pltpu.SMEM((slots,), jnp.int32),
            pltpu.SMEM((1, 1), jnp.int32),
            vmem((slots + 1, block, block), BF16),
            vmem((width, width), BF16),
            vmem((nodes, width), BF16),
            vmem((FEATS, rows, nodes, fw), BF16),
            vmem((PARTS, 2, half, sub, depth), BF16),
            vmem((PARTS, 2, groups, depth, group * sub), BF16),
            vmem((PARTS, FEATS, half, sub, fw), BF16),
            vmem((PARTS, FEATS, half, sub, fw), BF16),
            vmem((PARTS, FEATS, half, sub, fw), F32),
            vmem((PARTS, FEATS, half, sub, fw), BF16),
            vmem((PARTS, FEATS, half, sub, fw), BF16),
            vmem((PARTS, FEATS, sub, fw), F32),
            vmem((FEATS, PARTS, 2, half, sub, fw), BF16),
            vmem((FEATS, depth, fw), F32),
            vmem((width, width), F32),
            vmem((plane, piece, width), BF16),
            vmem((plane, piece, width), BF16),
            vmem((half, piece, width), BF16),
            vmem((plane, piece, width), BF16),
            vmem((FEATS, rows, nodes, fw), BF16),
            vmem((FEATS, rows, nodes, fw), BF16),
            dma((sum(counts(rows, cols).values()),)),
        ],
        compiler_params=pltpu.CompilerParams(collective_id=0, has_side_effects=True),
    )(
        block_position.reshape(slots),
        tile_count,
        node_features,
        layer_weight,
        output_grad,
        block_values.reshape(slots, block, block),
    )
    return pl.pallas_call(
        finish,
        out_shape=shapes,
        in_specs=[inside] * 3,
        out_specs=(place,) * 3,
        scratch_shapes=[
            dma((3,)),
        ],
        compiler_params=pltpu.CompilerParams(vmem_limit_bytes=4 << 20),
    )(*results)


def solution(mesh):
    in_specs = (
        P(("row", "col"), None),
        P(),
        P(("row", "col"), None),
        P("row", "col", None, None, None),
        P("row", "col", None),
        P("row", "col"),
    )
    out_specs = (P(("row", "col"), None), P(("row", "col"), None), P())
    return jax.shard_map(body, mesh=mesh, in_specs=in_specs, out_specs=out_specs, check_vma=False)
```

```python
import functools
import math

import jax
import jax.numpy as jnp
from jax import lax
from jax.experimental import pallas as pl
from jax.experimental.pallas import tpu as pltpu
from jax.sharding import PartitionSpec as P

MESH = pl.DeviceIdType.MESH
F32 = jnp.float32
BF16 = jnp.bfloat16
PARTS = 2
FEATS = 2
LEADS = (96, 64)


def repeat(steps, step):
    if len(steps) <= 8:
        for d in steps:
            step(d)
    elif len(steps) > 0:

        def one(d, unused):
            step(d)
            return unused

        lax.fori_loop(min(steps), max(steps) + 1, one, 0)


def split_dot(left, right, dims):
    high = left.astype(BF16)
    low = (left - high.astype(F32)).astype(BF16)
    first = lax.dot_general(high, right, dims, preferred_element_type=F32)
    return first + lax.dot_general(low, right, dims, preferred_element_type=F32)


def counts(rows, cols):
    half = cols // 2
    return {
        "load": 5 + FEATS,
        "x_mate": FEATS,
        "x_lead": FEATS,
        "x_rest": FEATS,
        "x_pass": FEATS,
        "yc": PARTS * FEATS * (half // 2),
        "yb": PARTS * (half // 2),
        "rz": PARTS,
        "gz": (1 + FEATS) * (half - 1),
        "gy": 1 + FEATS,
        "c": FEATS,
        "w": 3,
        "s_x": 1,
        "s_ry": 1,
        "s_rz": 1,
        "s_gz": 1,
        "s_gy": 1,
        "s_c": 1,
        "s_w": 3,
    }


EARLY = ("load", "x_mate", "x_lead", "x_rest", "x_pass", "yc", "yb", "rz", "s_x", "s_ry", "s_rz")


def kernel(
    rows,
    cols,
    position_hbm,
    count_hbm,
    x_hbm,
    w_hbm,
    og_hbm,
    values_hbm,
    out_ref,
    ig_ref,
    wg_ref,
    position,
    count,
    values,
    w_ref,
    og_ref,
    xg,
    tile,
    tile_t,
    mate_part,
    mate_in,
    own,
    part,
    part_in,
    keep,
    up,
    acc,
    term_sum,
    term,
    w1_in,
    w2_in,
    w3_in,
    pc,
    pc_in,
    sems,
):
    scope = jax.named_scope
    nodes, width = x_hbm.shape
    slots, block = values_hbm.shape[0], values_hbm.shape[1]
    col_blocks = rows
    my_row = lax.axis_index("row")
    my_col = lax.axis_index("col")
    half = cols // 2
    exts = rows // 2
    high = my_col // 2
    low = lax.rem(my_col, 2)
    mate = high * 2 + 1 - low
    ext = my_row // 2
    core = lax.rem(my_row, 2)
    core_mate = ext * 2 + 1 - core
    plane = 2 * rows
    my_spot = my_row * 2 + low
    sub = nodes // PARTS
    fw = width // FEATS
    leads = [nodes * LEADS[f] // 128 for f in range(FEATS)]
    group = min(half, 4)
    groups = half // group
    wing = half // 2
    side = high // wing
    rank = lax.rem(high, wing)
    ext_steps = list(range(1, exts))
    lead_rows = [pl.ds(0, n) for n in leads]
    rest_rows = [pl.ds(n, nodes - n) for n in leads]

    base, total = {}, {True: 0, False: 0}
    for name, size in counts(rows, cols).items():
        base[name] = total[name in EARLY]
        total[name in EARLY] += size
    arrays = {False: sems}

    def sem(name, index=0):
        return arrays[name in EARLY].at[base[name] + index]

    def across(step):
        def one(j):
            far = (1 - side) * wing + lax.rem(wing - 1 - rank + j, wing)
            step(j, far, far)

        repeat(list(range(wing)), one)

    def beside(step):
        def one(j):
            to = side * wing + lax.rem(rank + j, wing)
            come = side * wing + lax.rem(rank + wing - j, wing)
            step(wing - 1 + j, to, come)

        repeat(list(range(1, wing)), one)

    def far_first(step):
        across(step)
        beside(step)

    def near_first(step):
        beside(step)
        across(step)

    def ext_ahead(d):
        return lax.rem(ext + d, exts)

    def ext_behind(d):
        return lax.rem(ext + exts - d, exts)

    def spot_ahead(d):
        return lax.rem(my_spot + d, plane)

    def move(src, dst, sent, got, **target):
        return pltpu.make_async_remote_copy(
            src_ref=src,
            dst_ref=dst,
            send_sem=sent,
            recv_sem=got,
            device_id=target,
            device_id_type=MESH,
        )

    def arrived(ref, got):
        move(ref, ref, sem("s_c"), got, col=mate).wait_recv()

    def gone(ref, sent):
        move(ref, ref, sent, sem("c"), col=mate).wait_send()

    def repeat_all(count, step):
        if count == 1:
            step(0)
        else:

            def one(g, unused):
                step(g)
                return unused

            lax.fori_loop(0, count, one, 0)

    def to_spots(src, dst, sent, got):
        def one(d):
            spot = spot_ahead(d)
            move(
                src(spot), dst.at[my_spot], sent, got,
                row=spot // 2, col=high * 2 + lax.rem(spot, 2),
            ).start()

        repeat(list(range(1, plane)), one)

    scale = 1.0 / math.sqrt(nodes * rows * cols)
    piece = width // plane
    over_nodes = (((0,), (0,)), ((), ()))
    both = pl.ds(0, FEATS)

    depth = rows * nodes

    def first_half(early):
        arrays[True] = early
        load = pltpu.make_async_copy(values_hbm, values.at[pl.ds(0, slots)], sem("load", 0))
        load_x = [
            pltpu.make_async_copy(
                x_hbm.at[:, pl.ds(f * fw, fw)], xg.at[f, my_row], sem("load", 5 + f)
            )
            for f in range(FEATS)
        ]
        load_w = pltpu.make_async_copy(w_hbm, w_ref, sem("load", 2))
        load_og = pltpu.make_async_copy(og_hbm, og_ref, sem("load", 3))
        load_position = pltpu.make_async_copy(position_hbm, position, sem("load", 4))
        load_count = pltpu.make_async_copy(count_hbm, count, sem("load", 1))
        for one in (*load_x, load_position, load_count, load, load_w, load_og):
            one.start()

        barrier = pltpu.get_barrier_semaphore()

        def greet(**target):
            pl.semaphore_signal(barrier, inc=1, device_id=target, device_id_type=MESH)

        far_first(lambda t, to, come: greet(col=to * 2 + low))

        def greet_spot(d):
            spot = spot_ahead(d)
            greet(row=spot // 2, col=high * 2 + lax.rem(spot, 2))

        repeat(list(range(1, plane)), greet_spot)
        values[slots] = jnp.zeros((block, block), BF16)
        for one in load_x:
            one.wait()
        with scope("bar"):
            pl.semaphore_wait(barrier, plane - 1 + half - 1)

        def x_send(f):
            mine = xg.at[f, my_row]

            def send_lead(d):
                move(
                    mine.at[lead_rows[f]], mine.at[lead_rows[f]], sem("s_x"), sem("x_lead", f),
                    row=ext_ahead(d) * 2 + core,
                ).start()

            def send_rest(d):
                for to in (core, 1 - core):
                    move(
                        mine.at[rest_rows[f]], mine.at[rest_rows[f]], sem("s_x"), sem("x_rest", f),
                        row=ext_ahead(d) * 2 + to,
                    ).start()

            if leads[f] > 0:
                repeat(ext_steps, send_lead)
            move(mine, mine, sem("s_x"), sem("x_mate", f), row=core_mate).start()
            repeat(ext_steps, send_rest)

        for f in range(FEATS):
            x_send(f)

        with scope("load"):
            load_position.wait()
            load_count.wait()
            load.wait()
        live_count = count[0, 0]

        def build(q, y, z, pointer):
            for k in range(col_blocks):
                here = position[jnp.minimum(pointer, slots - 1)]
                live = (here == q * col_blocks + k) & (pointer < live_count)
                value = values[jnp.where(live, pointer, slots)]
                for p in range(PARTS):
                    tile[p, y, z, :, pl.ds(k * block, block)] = value[p * sub : (p + 1) * sub, :]
                pointer = pointer + live.astype(jnp.int32)
            return pointer

        with scope("build"):
            if cols <= 8:
                pointer = jnp.int32(0)
                for q in range(cols):
                    pointer = build(q, q % 2, q // 2, pointer)
            else:

                def build_pair(z, pointer):
                    for y in range(2):
                        pointer = build(z * 2 + y, y, z, pointer)
                    return pointer

                lax.fori_loop(0, half, build_pair, jnp.int32(0))

        def x_relay(f):
            if leads[f] == 0:
                return
            with scope("x_lead%d" % f):
                arrived(xg.at[f, pl.ds(0, exts - 1), lead_rows[f]], sem("x_lead", f))

            def one(d):
                slot = xg.at[f, ext_behind(d) * 2 + core, lead_rows[f]]
                move(slot, slot, sem("s_x"), sem("x_pass", f), row=core_mate).start()

            repeat(ext_steps, one)

        def x_wait(f):
            with scope("x_rest%d" % f):
                arrived(xg.at[f, 0], sem("x_mate", f))
                arrived(xg.at[f, pl.ds(0, 2 * (exts - 1)), rest_rows[f]], sem("x_rest", f))
            if leads[f] == 0:
                return
            with scope("x_pass%d" % f):
                arrived(xg.at[f, pl.ds(0, exts - 1), lead_rows[f]], sem("x_pass", f))

        def product(p, f, y, g):
            left = tile[p, y, pl.ds(g * group, group)].reshape(group * sub, depth)
            panel = xg[f].reshape(depth, fw)
            return jnp.dot(left, panel, preferred_element_type=F32).reshape(group, sub, fw)

        def yc(p, f, j):
            return sem("yc", (p * FEATS + f) * wing + j)

        def yb(p, j):
            return sem("yb", p * wing + j)

        def for_mate(p, f):
            def one(g):
                mate_part[p, f, pl.ds(g * group, group)] = product(p, f, 1 - low, g).astype(BF16)

            repeat_all(groups, one)

            def send(j, z, unused):
                move(
                    mate_part.at[p, f, z], mate_in.at[p, f, z], sem("s_ry"), yc(p, f, j), col=mate
                ).start()

            across(send)

        def for_mate_near(p):
            def send(t, z, unused):
                move(
                    mate_part.at[p, :, z], mate_in.at[p, :, z], sem("s_ry"), yb(p, t - wing), col=mate
                ).start()

            beside(send)
            send(2 * wing - 1, high, high)

        def for_me(p, f):
            def one(g):
                own[p, f, pl.ds(g * group, group)] = product(p, f, low, g)

            repeat_all(groups, one)

        x_relay(0)
        x_wait(0)
        with scope("fwd0"):
            for_mate(0, 0)
        for f in range(1, FEATS):
            x_relay(f)
        for f in range(1, FEATS):
            x_wait(f)
            for_mate(0, f)
        with scope("fwd1"):
            for p in range(1, PARTS):
                for f in range(FEATS):
                    for_mate(p, f)
            for p in range(PARTS):
                for_mate_near(p)
            for p in range(PARTS):
                for f in range(FEATS):
                    for_me(p, f)

        def turn(p, y):
            def one(g):
                for k in range(col_blocks):
                    left = tile[p, y, pl.ds(g * group, group), :, pl.ds(k * block, block)]
                    tile_t[p, y, g, pl.ds(k * block, block), :] = left.reshape(group * sub, block).T

            repeat_all(groups, one)

        with scope("turn"):
            for p in range(PARTS):
                for y in range(2):
                    turn(p, y)

        def to_across(p, f):
            def one(j, z, unused):
                arrived(mate_in.at[p, f, z], yc(p, f, j))
                part[p, f, z] = (own[p, f, z] + mate_in[p, f, z].astype(F32)).astype(BF16)
                move(
                    part.at[p, f, z], part_in.at[p, f, high], sem("s_rz"), sem("rz", p),
                    col=z * 2 + low,
                ).start()

            across(one)

        def to_beside(p):
            def one(t, z, unused):
                arrived(mate_in.at[p, :, z], yb(p, t - wing))
                part[p, :, z] = (own[p, :, z] + mate_in[p, :, z].astype(F32)).astype(BF16)
                move(
                    part.at[p, :, z], part_in.at[p, :, high], sem("s_rz"), sem("rz", p),
                    col=z * 2 + low,
                ).start()

            beside(one)
            arrived(mate_in.at[p, :, high], yb(p, wing - 1))
            keep[p] = own[p, :, high] + mate_in[p, :, high].astype(F32)

        for p in range(PARTS):
            for f in range(FEATS):
                with scope("across%d%d" % (p, f)):
                    to_across(p, f)
        for p in range(PARTS):
            with scope("beside%d" % p):
                to_beside(p)

        load_w.wait()
        load_og.wait()
        def spread(f, p, index):
            mine = up.at[f, p, low, high]
            far_first(
                lambda t, z, unused: move(
                    mine, mine, sem("s_gz"), sem("gz", index * (half - 1) + t), col=z * 2 + low
                ).start()
            )
            move(mine, mine, sem("s_gy"), sem("gy", index), col=mate).start()

        def middle(p):
            with scope("rz%d" % p):
                arrived(part_in.at[p, :, pl.ds(0, half - 1)], sem("rz", p))

            def add(t, unused, z):
                keep[p] += part_in[p, :, z].astype(F32)

            near_first(add)
            mixed = jnp.concatenate([keep[p, f] for f in range(FEATS)], axis=1)
            pre = split_dot(mixed, w_ref[...], (((1,), (0,)), ((), ())))
            decay = jnp.exp(jnp.minimum(pre, 0.0))
            slope = jnp.where(pre > 0, 1.0, decay)
            some = pl.ds(p * sub, sub)
            upstream = (og_ref[some].astype(F32) * slope).astype(BF16)
            for f in range(FEATS):
                up[f, p, low, high] = upstream[:, f * fw : (f + 1) * fw]
            if p < PARTS - 1:
                spread(both, p, 0)
            else:
                for f in range(FEATS):
                    spread(f, p, 1 + f)
            out_ref[some] = jnp.where(pre > 0, pre, decay - 1.0).astype(BF16)
            share = split_dot(mixed, upstream, over_nodes)
            if p == 0:
                term_sum[...] = share
            else:
                share = term_sum[...] + share
                term[...] = (share * scale).reshape(plane, piece, width).astype(BF16)

        for p in range(PARTS):
            with scope("middle%d" % p):
                middle(p)

        with scope("w1_send"):
            to_spots(lambda spot: term.at[spot], w1_in, sem("s_w", 0), sem("w", 0))
            w1_in[my_spot] = term[my_spot]
        with scope("gone_early"):
            gone(xg.at[:, pl.ds(0, rows - 1)], sem("s_x"))
            gone(mate_part, sem("s_ry"))
            gone(part.at[:, :, pl.ds(0, half - 1)], sem("s_rz"))

    pl.run_scoped(first_half, pltpu.SemaphoreType.DMA((total[True],)))

    def region(f, p, z):
        return up.at[f, p, low, z]

    def pass_on(f, p, index):
        def one(t, unused, z):
            slot = region(f, p, z)
            arrived(slot, sem("gz", index * (half - 1) + t))
            move(slot, slot, sem("s_gy"), sem("gy", index), col=mate).start()

        near_first(one)

    def back(f, p, y, first=False):
        def one(g):
            right = up[f, p, y, pl.ds(g * group, group)].reshape(group * sub, fw)
            got = jnp.dot(tile_t[p, y, g], right, preferred_element_type=F32)
            if first:
                acc[f] = got
            else:
                acc[f] += got

        if first and groups > 1:
            acc[f] = jnp.zeros(acc.shape[1:], F32)
            first = False
        repeat_all(groups, one)

    with scope("gz_p0"):
        pass_on(both, 0, 0)
    for f in range(FEATS):
        back(f, 0, low, first=True)
    for f in range(FEATS):
        with scope("gz_p1_%d" % f):
            pass_on(f, 1, 1 + f)
    with scope("w1_wait"):
        arrived(w1_in.at[pl.ds(0, plane - 1)], sem("w", 0))
        w2_in[high] = jnp.sum(w1_in[...].astype(F32), axis=0).astype(BF16)
        far_first(
            lambda t, z, unused: move(
                w2_in.at[high], w2_in.at[high], sem("s_w", 1), sem("w", 1), col=z * 2 + low
            ).start()
        )
    for f in range(FEATS):
        back(f, 1, low)

    with scope("gy_p0"):
        arrived(up.at[both, 0, 1 - low], sem("gy", 0))
    for f in range(FEATS):
        back(f, 0, 1 - low)

    def block_of(r):
        return pl.ds(pl.multiple_of(r * nodes, nodes), nodes)

    def launch(f):
        def one(r):
            pc[f, r] = acc[f, block_of(r)].astype(BF16)
            move(pc.at[f, r], pc_in.at[f, my_row], sem("s_c"), sem("c", f), row=r).start()

        def outside(d):
            one(ext_ahead(d) * 2 + core)
            one(ext_ahead(d) * 2 + 1 - core)

        repeat(ext_steps, outside)
        one(core_mate)

    def gather_grad(f):
        arrived(pc_in.at[f, pl.ds(0, rows - 1)], sem("c", f))

        def add(r):
            acc[f, block_of(my_row)] += pc_in[f, r].astype(F32)

        def outside(d):
            for k in range(2):
                add(ext_behind(d) * 2 + k)

        repeat(ext_steps, outside)
        add(core_mate)
        some = pl.ds(f * fw, fw)
        return split_dot(acc[f, block_of(my_row)], w_ref[:, some], (((1,), (1,)), ((), ())))

    for f in range(FEATS):
        with scope("gy_p1_%d" % f):
            arrived(up.at[f, 1, 1 - low], sem("gy", 1 + f))
        back(f, 1, 1 - low)
        with scope("launch%d" % f):
            launch(f)
    with scope("w2_wait"):
        arrived(w2_in.at[pl.ds(0, half - 1)], sem("w", 1))
        w3_in[my_spot] = jnp.sum(w2_in[...].astype(F32), axis=0).astype(BF16)
        to_spots(lambda spot: w3_in.at[my_spot], w3_in, sem("s_w", 2), sem("w", 2))
    grad = 0.0
    for f in range(FEATS):
        with scope("grad%d" % f):
            grad = grad + gather_grad(f)
    ig_ref[...] = grad.astype(BF16)

    with scope("gone"):
        gone(up.at[:, :, low, pl.ds(0, half - 1)], sem("s_gz"))
        gone(up.at[:, :, low], sem("s_gy"))
        gone(pc.at[:, pl.ds(0, rows - 1)], sem("s_c"))
        gone(term.at[pl.ds(0, plane - 1)], sem("s_w", 0))
        gone(w2_in.at[pl.ds(0, half - 1)], sem("s_w", 1))
        gone(w3_in.at[pl.ds(0, plane - 1)], sem("s_w", 2))
    with scope("w3_wait"):
        arrived(w3_in.at[pl.ds(0, plane - 1)], sem("w", 2))
    wg_ref[...] = w3_in[...].reshape(width, width).astype(F32)


def finish(out_ref, ig_ref, wg_ref, out_hbm, ig_hbm, wg_hbm, sem):
    trio = ((out_ref, out_hbm), (ig_ref, ig_hbm), (wg_ref, wg_hbm))
    copies = [pltpu.make_async_copy(a, b, sem.at[i]) for i, (a, b) in enumerate(trio)]
    for copy in copies:
        copy.start()
    for copy in copies:
        copy.wait()


def body(node_features, layer_weight, output_grad, block_values, block_position, tile_count):
    rows, cols = lax.axis_size("row"), lax.axis_size("col")
    nodes, width = node_features.shape
    slots, block = block_values.shape[2], block_values.shape[3]
    half, exts, plane = cols // 2, rows // 2, 2 * rows
    assert nodes == block and cols == 2 * half and rows == 2 * exts
    sub, fw = nodes // PARTS, width // FEATS
    group = min(half, 4)
    groups = half // group
    piece = width // plane
    depth = rows * nodes
    place = pl.BlockSpec(memory_space=pl.ANY)
    pinned = pl.BlockSpec(memory_space=pltpu.HBM)
    inside = pl.BlockSpec(memory_space=pltpu.VMEM)
    dma = pltpu.SemaphoreType.DMA
    vmem = pltpu.VMEM
    shapes = (
        jax.ShapeDtypeStruct((nodes, width), BF16),
        jax.ShapeDtypeStruct((nodes, width), BF16),
        jax.ShapeDtypeStruct((width, width), F32),
    )
    results = pl.pallas_call(
        functools.partial(kernel, rows, cols),
        out_shape=(
            vmem((nodes, width), BF16),
            vmem((nodes, width), BF16),
            vmem((width, width), F32),
        ),
        in_specs=[pinned, pinned, place, place, place, place],
        out_specs=(inside, inside, inside),
        scratch_shapes=[
            pltpu.SMEM((slots,), jnp.int32),
            pltpu.SMEM((1, 1), jnp.int32),
            vmem((slots + 1, block, block), BF16),
            vmem((width, width), BF16),
            vmem((nodes, width), BF16),
            vmem((FEATS, rows, nodes, fw), BF16),
            vmem((PARTS, 2, half, sub, depth), BF16),
            vmem((PARTS, 2, groups, depth, group * sub), BF16),
            vmem((PARTS, FEATS, half, sub, fw), BF16),
            vmem((PARTS, FEATS, half, sub, fw), BF16),
            vmem((PARTS, FEATS, half, sub, fw), F32),
            vmem((PARTS, FEATS, half, sub, fw), BF16),
            vmem((PARTS, FEATS, half, sub, fw), BF16),
            vmem((PARTS, FEATS, sub, fw), F32),
            vmem((FEATS, PARTS, 2, half, sub, fw), BF16),
            vmem((FEATS, depth, fw), F32),
            vmem((width, width), F32),
            vmem((plane, piece, width), BF16),
            vmem((plane, piece, width), BF16),
            vmem((half, piece, width), BF16),
            vmem((plane, piece, width), BF16),
            vmem((FEATS, rows, nodes, fw), BF16),
            vmem((FEATS, rows, nodes, fw), BF16),
            dma((sum(n for name, n in counts(rows, cols).items() if name not in EARLY),)),
        ],
        compiler_params=pltpu.CompilerParams(collective_id=0, has_side_effects=True),
    )(
        block_position.reshape(slots),
        tile_count,
        node_features,
        layer_weight,
        output_grad,
        block_values.reshape(slots, block, block),
    )
    return pl.pallas_call(
        finish,
        out_shape=shapes,
        in_specs=[inside] * 3,
        out_specs=(place,) * 3,
        scratch_shapes=[
            dma((3,)),
        ],
        compiler_params=pltpu.CompilerParams(vmem_limit_bytes=4 << 20),
    )(*results)


def solution(mesh):
    in_specs = (
        P(("row", "col"), None),
        P(),
        P(("row", "col"), None),
        P("row", "col", None, None, None),
        P("row", "col", None),
        P("row", "col"),
    )
    out_specs = (P(("row", "col"), None), P(("row", "col"), None), P())
    return jax.shard_map(body, mesh=mesh, in_specs=in_specs, out_specs=out_specs, check_vma=False)
```
